128 devices in a mesh: src: 32 (over y, x_hi, z), sta: 4 (over x_lo, core).
Axes of the slice: x: 4 (x_hi: 2, x_lo: 2; x = x_hi * 2 + x_lo), y: 4, z: 4, core: 2. Of those that a mesh axis runs over, the one named last changes fastest.
Arguments:
- trace: float32 [256, 8256], P('sta', 'src'), may hold values from -6 to 6
- quadrature: float32 [256, 8256], P('sta', 'src'), may hold values from -6 to 6
- gains: float32 [256], P('sta'), may hold values from 0.3 to 3
- lags: int32 [4096, 256], P('src', 'sta'), may hold values from 0 to 63
Outputs:
- beam_power: float32 [2, 4096], P(None, 'src')
The draws below stay inside these ranges and needn't reach their ends.
All inputs are finite; a program needn't handle non-finite values.
Results may differ from the reference program's by a relative error of at most 0.0003.
Values may be sent and summed in bfloat16 or wider, within the bound.
No kernel may reach another device: no remote copies, remote signals or barrier semaphores. Data moves between devices by JAX's collectives and lax.ppermute only.
A program may use at most 256 MiB of HBM per device.

```python
import math
import jax
import jax.numpy as jnp
from jax import lax

W = 4096
LAGS = 64
STEPS = 2
NT = 8256
S = 256
C = 4096


def set_ends(values, stream_key, low, top_value):
    extent = values.shape
    index_at = [jax.random.randint(jax.random.fold_in(stream_key, axis), (), 0, extent[axis]) for axis in range(len(extent))]
    values = values.at[tuple(index_at)].set(low)
    longest = extent.index(max(extent))
    index_at[longest] = (index_at[longest] + 1) % extent[longest]
    return values.at[tuple(index_at)].set(top_value)


def steps_of(rng, shape, split, low, largest):
    level, own = 1.0, jax.random.fold_in(rng, 6)
    for dim, blocks in split:
        heights = jnp.exp(jax.random.uniform(jax.random.fold_in(own, dim), (blocks,), jnp.float32, low / len(split), largest / len(split)))
        level = level * jnp.repeat(heights, shape[dim] // blocks).reshape([-1 if axis == dim else 1 for axis in range(len(shape))])
    return level


def bell_draw(key, shape, deviation, limit, shards=(), held_as=jnp.bfloat16):
    values = jax.random.normal(key, shape, jnp.float32) * deviation
    if len(shards) > 0:
        values = steps_of(key, shape, shards, -0.22, 0.18) * values
    return jnp.clip(values, min=-limit, max=limit).astype(held_as)


def setup_inputs(seed: int = 0) -> dict:
    keys = jax.random.split(jax.random.key(seed), 5)
    trace = bell_draw(keys[0], (S, NT), 1.0, 6.0, ((0, 4), (1, 32)), jnp.float32)
    quadrature = bell_draw(keys[1], (S, NT), 1.0, 6.0, ((0, 4), (1, 32)), jnp.float32)
    gains = jnp.clip(jnp.exp(math.log(3.0) - 2.3025851 * jax.random.uniform(keys[2], (S,), jnp.float32) ** steps_of(keys[2], (S,), ((0, 4),), -0.2, 0.2)), 0.3, 3.0)
    lags = set_ends(jax.random.randint(keys[3], (C, S), 0, LAGS), jax.random.fold_in(keys[3], 1), 0, LAGS - 1).astype(jnp.int32)
    return dict(trace=trace, quadrature=quadrature, gains=gains, lags=lags)


def reference(trace, quadrature, gains, lags):
    energy = trace * trace + quadrature * quadrature
    baseline = jnp.mean(energy, axis=1, keepdims=True)
    weighted = (gains[:, None] * (energy - baseline)).astype(jnp.bfloat16)
    weighted_wide = weighted.astype(jnp.float32)
    cell_total = lags.shape[0]
    power_rows = []
    for step_index in range(STEPS):
        def add_lag(summed, lag_value):
            selector = (lags == lag_value).astype(jnp.float32)
            window = lax.dynamic_slice_in_dim(weighted_wide, (step_index * W + lag_value).astype(jnp.int32), W, 1)
            return summed + jnp.dot(selector, window, precision=lax.Precision.HIGHEST), None

        beam, unused = lax.scan(add_lag, jnp.zeros((cell_total, W), jnp.float32), jnp.arange(LAGS, dtype=jnp.int32))
        power_rows.append(jnp.sum(beam * beam, axis=1))
    power = jnp.stack(power_rows)
    return power / jnp.max(power, axis=1, keepdims=True)
```

```python
import functools

import jax
import jax.numpy as jnp
from jax import lax
from jax.experimental import pallas as pl
from jax.experimental.pallas import tpu as pltpu
from jax.sharding import PartitionSpec as P

W = 4096
LAGS = 64
STEPS = 2
F32 = jnp.float32
BF16 = jnp.bfloat16
VMEM = pl.BlockSpec(memory_space=pltpu.VMEM)
SMEM = pl.BlockSpec(memory_space=pltpu.SMEM)

SRC = 32
STA = 4
DEV = SRC * STA
BLK = 258
ST = 64
STATIONS = ST * STA
WIN = 256
CPD = 128
ROWS = 24
SAMPLES = BLK * SRC
HALF = SRC // STEPS * STA


def prologue(where, trace, quad, gains, lags, own, left, right, chunk):
    tr, qd = trace[...], quad[...]
    energy = tr * tr + qd * qd
    own[:, :BLK] = energy
    own[:, BLK:] = jnp.broadcast_to(gains[...], (ST, 384 - BLK))
    left[...] = energy[:, BLK - 128 :]
    right[...] = energy[:, :128]
    total = jnp.sum(energy, axis=1, keepdims=True)
    total = jnp.broadcast_to(total, (ST, 128))
    total = jnp.concatenate([total, total], axis=0).T[:8]
    hi = total.astype(BF16).astype(F32)
    mid = (total - hi).astype(BF16).astype(F32)
    low = total - hi - mid
    row = lax.broadcasted_iota(jnp.int32, (8, 128), 0)
    lane = lax.broadcasted_iota(jnp.int32, (8, 128), 1)
    sums = jnp.where(row == 0, hi, jnp.where(row == 1, mid, jnp.where(row == 2, low, 0.0)))
    sums = jnp.where(lane // ST == where[1] % 2, sums, 0.0)
    for j in range(STA):
        first = lags[32 * j : 32 * j + 16, :]
        second = lags[32 * j + 16 : 32 * j + 32, :]
        body = jnp.concatenate([first, second], axis=1).astype(F32)
        chunk[j] = jnp.concatenate([body, sums], axis=0).astype(BF16)


def window(where, e0, e1, e2, e3, h0, h1, h2, h3, win, gains, tall, edges, line):
    for k, (e, h) in enumerate(((e0, h0), (e1, h1), (e2, h2), (e3, h3))):
        at = pl.multiple_of((where[1] + k) % STA * ST, ST)
        tall[pl.ds(at, ST), :] = e[...]
        edges[pl.ds(at, ST), :] = h[...]
    side = edges[...].T
    main = tall[...].T
    line[64:448, :] = main
    line[0:64, :] = side[64:128]
    line[64 + BLK : 64 + BLK + 64, :] = side[0:64]
    win[...] = pltpu.roll(line[...], 448 - 64 + 2 * where[0], 0)[:320]
    gains[...] = jnp.broadcast_to(main[BLK : BLK + 1], (8, STATIONS))


def beams(received, win, gains, power, weighted, lagged):
    halves = []
    for half in range(2):
        acc = jnp.zeros((8, 128), F32)
        for i in range(SRC):
            for j in (2 * half, 2 * half + 1):
                acc = acc + received[STA * i + j, 16:24, :].astype(F32)
        halves.append(jnp.sum(acc, axis=0, keepdims=True))
    baseline = jnp.concatenate(halves, axis=1) / SAMPLES
    gain = gains[0:1, :]
    for b in range(16):
        rows = 304 if b < 15 else 304
        weighted[b] = (gain * (win[b : b + rows, :] - baseline)).astype(BF16)
    for j in range(STA):
        part = jnp.concatenate([received[STA * i + j, 0:16, :] for i in range(SRC)], axis=0)
        part = part.astype(F32).T.astype(BF16)
        for h in range(2):
            lagged[h, ST * j : ST * j + ST, :] = part[ST * h : ST * h + ST]
    for group in range(4):
        cols = slice(256 * (group % 2), 256 * (group % 2) + 256)

        def add(step, total):
            base = pl.multiple_of(step * 16, 16)
            picks, shifted = [], []
            lag = lagged[group // 2, :, cols]
            for b in range(16):
                value = (base + b).astype(F32).astype(BF16)
                picks.append(jnp.where(lag == value, BF16(1), BF16(0)))
                shifted.append(weighted[b, pl.ds(base, WIN), :])
            return total + jnp.dot(
                jnp.concatenate(shifted, axis=1), jnp.concatenate(picks, axis=0), preferred_element_type=F32
            )

        beam = lax.fori_loop(0, LAGS // 16, add, jnp.zeros((WIN, 256), F32))
        squared = jnp.sum(beam * beam, axis=0, keepdims=True)
        power[2 * group : 2 * group + 1, :] = squared[:, :128]
        power[2 * group + 1 : 2 * group + 2, :] = squared[:, 128:]


def finish(where, parts, out, sums):
    src = where[0]
    lane = lax.broadcasted_iota(jnp.int32, (1, 128), 1)
    for k in range(STEPS):
        peak = None
        for j in range(STA):
            acc = parts[k * HALF + j]
            for i in range(1, SRC // STEPS):
                acc = acc + parts[k * HALF + STA * i + j]
            sums[8 * j : 8 * j + 8, :] = acc
            peak = acc if peak is None else jnp.maximum(peak, acc)
        peak = jnp.max(peak, axis=(0, 1), keepdims=True)
        cells = jnp.zeros((1, 128), F32)
        for j in range(STA):
            for h in range(2):
                row = sums[pl.ds(8 * j + 4 * h + src // 8, 1), :]
                to = 32 * j + 16 * h
                row = pltpu.roll(row, (to - 16 * (src % 8)) % 128, 1)
                cells = jnp.where(lane // 16 == to // 16, row, cells)
        out[k : k + 1, :] = cells / peak


def call(kernel, out_shape, specs, scratch=(), name=None):
    multi = isinstance(out_shape, (list, tuple))
    return pl.pallas_call(
        kernel,
        out_shape=out_shape,
        in_specs=specs,
        out_specs=[VMEM] * len(out_shape) if multi else VMEM,
        scratch_shapes=scratch,
        compiler_params=pltpu.CompilerParams(vmem_limit_bytes=48 << 20),
        name=name,
    )


def shape(dims, dtype=F32):
    return jax.ShapeDtypeStruct(dims, dtype)


def on_device(trace, quadrature, gains, lags):
    where = jnp.stack([lax.axis_index("src"), lax.axis_index("sta")]).astype(jnp.int32)
    own, left, right, chunk = call(
        prologue,
        [shape((ST, 384)), shape((ST, 128)), shape((ST, 128)), shape((STA, ROWS, 128), BF16)],
        [SMEM] + [VMEM] * 4,
        name="prologue",
    )(where, trace, quadrature, gains[:, None], lags)
    chunks = jnp.broadcast_to(chunk[None], (SRC, STA, ROWS, 128)).reshape(DEV, ROWS, 128)
    received = lax.all_to_all(chunks, ("src", "sta"), 0, 0, tiled=True)

    def from_sta(x, k):
        return lax.ppermute(x, "sta", [((j + k) % STA, j) for j in range(STA)])

    blocks = [own] + [from_sta(own, k) for k in range(1, STA)]
    before = lax.ppermute(left, "src", [(i, (i + 1) % SRC) for i in range(SRC)])
    after = lax.ppermute(right, "src", [((i + 1) % SRC, i) for i in range(SRC)])
    edge = jnp.where(jnp.arange(128)[None, :] < 64, after, before)
    edges = [edge] + [from_sta(edge, k) for k in range(1, STA)]
    win, gain = call(
        window,
        [shape((320, STATIONS)), shape((8, STATIONS))],
        [SMEM] + [VMEM] * 8,
        [pltpu.VMEM((STATIONS, 384), F32), pltpu.VMEM((STATIONS, 128), F32), pltpu.VMEM((448, STATIONS), F32)],
        name="window",
    )(where, *blocks, *edges)
    power = call(
        beams,
        shape((8, 128)),
        [VMEM] * 3,
        [pltpu.VMEM((16, 304, STATIONS), BF16), pltpu.VMEM((2, STATIONS, 512), BF16)],
        name="beams",
    )(received, win, gain)
    parts = lax.all_to_all(jnp.broadcast_to(power[None], (DEV, 8, 128)), ("src", "sta"), 0, 0, tiled=True)
    return call(finish, shape((STEPS, CPD)), [SMEM, VMEM], [pltpu.VMEM((32, 128), F32)], name="finish")(where, parts)


def solution(mesh):
    return jax.shard_map(
        on_device,
        mesh=mesh,
        in_specs=(P("sta", "src"), P("sta", "src"), P("sta"), P("src", "sta")),
        out_specs=P(None, "src"),
        check_vma=False,
    )
```

```python
import functools

import jax
import jax.numpy as jnp
from jax import lax
from jax.experimental import pallas as pl
from jax.experimental.pallas import tpu as pltpu
from jax.sharding import PartitionSpec as P

W = 4096
LAGS = 64
STEPS = 2
F32 = jnp.float32
BF16 = jnp.bfloat16
VMEM = pl.BlockSpec(memory_space=pltpu.VMEM)
SMEM = pl.BlockSpec(memory_space=pltpu.SMEM)

SRC = 32
STA = 4
DEV = SRC * STA
BLK = 258
ST = 64
STATIONS = ST * STA
HALO = LAGS - 1
ROWS_OUT = 272
ROWS_IN = ROWS_OUT + LAGS
CPD = 128
ROWS = 24
SAMPLES = BLK * SRC
HALF = SRC // STEPS * STA


def prologue(where, trace, quad, gains, lags, own, near, far, chunk, tr_in, qd_in, ga_in, lg_in, sem):
    copies = [
        pltpu.make_async_copy(a, b, sem.at[k])
        for k, (a, b) in enumerate(((trace, tr_in), (quad, qd_in), (gains, ga_in), (lags, lg_in)))
    ]
    for copy in copies:
        copy.start()
    for copy in copies:
        copy.wait()
    tr, qd = tr_in[...], qd_in[...]
    energy = tr * tr + qd * qd
    own[:, :BLK] = energy
    gain = jnp.concatenate([ga_in[...], ga_in[...]], axis=1)
    gain = jnp.broadcast_to(gain, (128, 128)).T[:ST]
    own[:, BLK:] = gain[:, : 384 - BLK]
    first, last = energy[:, :128], energy[:, BLK - 128 :]
    low_half = where[0] < SRC // STEPS
    near[...] = jnp.where(low_half, first, last)
    far[...] = jnp.where(low_half, last, first)
    total = jnp.sum(energy, axis=1, keepdims=True)
    total = jnp.broadcast_to(total, (ST, 128))
    total = jnp.concatenate([total, total], axis=0).T[:8]
    hi = total.astype(BF16).astype(F32)
    mid = (total - hi).astype(BF16).astype(F32)
    low = total - hi - mid
    row = lax.broadcasted_iota(jnp.int32, (8, 128), 0)
    lane = lax.broadcasted_iota(jnp.int32, (8, 128), 1)
    sums = jnp.where(row == 0, hi, jnp.where(row == 1, mid, jnp.where(row == 2, low, 0.0)))
    sums = jnp.where(lane // ST == where[1] % 2, sums, 0.0)
    lag = lg_in[...].astype(F32)
    lag = jnp.concatenate([lag, lag], axis=0).T
    for j in range(STA):
        body = jnp.where(lane[:1] < ST, lag[32 * j : 32 * j + 16], lag[32 * j + 16 : 32 * j + 32])
        chunk[j] = jnp.concatenate([body, sums], axis=0).astype(BF16)


def window(where, e0, e1, e2, e3, h0, h1, h2, h3, win, gains, tall, edges, line):
    for k, (e, h) in enumerate(((e0, h0), (e1, h1), (e2, h2), (e3, h3))):
        at = pl.multiple_of((where[1] + k) % STA * ST, ST)
        tall[pl.ds(at, ST), :] = e[...]
        edges[pl.ds(at, ST), :] = h[...]
    side = edges[...].T
    main = tall[...].T
    line[0:128, :] = side
    line[128:512, :] = main
    line[128 + BLK : 128 + BLK + 64, :] = side[0:64]
    ahead = line[128 : 128 + ROWS_IN, :]
    behind = line[128 - HALO : 128 - HALO + ROWS_IN, :]
    win[...] = jnp.where(where[0] < SRC // STEPS, ahead, behind)
    gains[...] = jnp.broadcast_to(main[BLK : BLK + 1], (8, STATIONS))


def beams(where, received, win, gains, power, weighted, lagged):
    halves = []
    for half in range(2):
        acc = jnp.zeros((8, 128), F32)
        for i in range(SRC):
            for j in (2 * half, 2 * half + 1):
                acc = acc + received[STA * i + j, 16:24, :].astype(F32)
        halves.append(jnp.sum(acc, axis=0, keepdims=True))
    baseline = jnp.concatenate(halves, axis=1) / SAMPLES
    gain = gains[0:1, :]
    for b in range(16):
        weighted[b] = (gain * (win[b : b + ROWS_OUT + 48, :] - baseline)).astype(BF16)
    src = where[0]
    start = jnp.where(src == SRC // STEPS, W - (BLK * (SRC // STEPS) - HALO), 0)
    stop = jnp.where(src == SRC // STEPS - 1, W - BLK * (SRC // STEPS - 1), jnp.where(src == SRC - 1, BLK - 1, BLK))
    row = lax.broadcasted_iota(jnp.int32, (ROWS_OUT, 256), 0)
    inside = jnp.logical_and(row >= start, row < stop)
    for j in range(STA):
        part = jnp.concatenate([received[STA * i + j, 0:16, :] for i in range(SRC)], axis=0)
        part = part.astype(F32).T.astype(BF16)
        for h in range(2):
            lagged[h, ST * j : ST * j + ST, :] = part[ST * h : ST * h + ST]
    for group in range(4):
        cols = slice(256 * (group % 2), 256 * (group % 2) + 256)

        def add(step, total):
            base = pl.multiple_of(step * 16, 16)
            picks, shifted = [], []
            lag = lagged[group // 2, :, cols]
            for b in range(16):
                value = (base + b).astype(F32).astype(BF16)
                picks.append(jnp.where(lag == value, BF16(1), BF16(0)))
                shifted.append(weighted[b, pl.ds(base, ROWS_OUT), :])
            return total + jnp.dot(
                jnp.concatenate(shifted, axis=1), jnp.concatenate(picks, axis=0), preferred_element_type=F32
            )

        beam = lax.fori_loop(0, LAGS // 16, add, jnp.zeros((ROWS_OUT, 256), F32))
        beam = jnp.where(inside, beam, 0.0)
        squared = jnp.sum(beam * beam, axis=0, keepdims=True)
        power[2 * group : 2 * group + 1, :] = squared[:, :128]
        power[2 * group + 1 : 2 * group + 2, :] = squared[:, 128:]


def finish(where, parts, out, sums):
    src = where[0]
    lane = lax.broadcasted_iota(jnp.int32, (1, 128), 1)
    for k in range(STEPS):
        peak = None
        for j in range(STA):
            acc = parts[k * HALF + j]
            for i in range(1, SRC // STEPS):
                acc = acc + parts[k * HALF + STA * i + j]
            sums[8 * j : 8 * j + 8, :] = acc
            peak = acc if peak is None else jnp.maximum(peak, acc)
        peak = jnp.max(peak, axis=(0, 1), keepdims=True)
        cells = jnp.zeros((1, 128), F32)
        for j in range(STA):
            for h in range(2):
                row = sums[pl.ds(8 * j + 4 * h + src // 8, 1), :]
                to = 32 * j + 16 * h
                row = pltpu.roll(row, (to - 16 * (src % 8)) % 128, 1)
                cells = jnp.where(lane // 16 == to // 16, row, cells)
        out[k : k + 1, :] = cells / peak


def call(kernel, out_shape, specs, scratch=(), name=None):
    multi = isinstance(out_shape, (list, tuple))
    return pl.pallas_call(
        kernel,
        out_shape=out_shape,
        in_specs=specs,
        out_specs=[VMEM] * len(out_shape) if multi else VMEM,
        scratch_shapes=scratch,
        compiler_params=pltpu.CompilerParams(vmem_limit_bytes=48 << 20),
        name=name,
    )


def shape(dims, dtype=F32):
    return jax.ShapeDtypeStruct(dims, dtype)


def on_device(trace, quadrature, gains, lags):
    where = jnp.stack([lax.axis_index("src"), lax.axis_index("sta")]).astype(jnp.int32)
    own, near, far, chunk = call(
        prologue,
        [shape((ST, 384)), shape((ST, 128)), shape((ST, 128)), shape((STA, ROWS, 128), BF16)],
        [SMEM] + [pl.BlockSpec(memory_space=pl.ANY)] * 4,
        [
            pltpu.VMEM((ST, BLK), F32),
            pltpu.VMEM((ST, BLK), F32),
            pltpu.VMEM((1, ST), F32),
            pltpu.VMEM((ST, CPD), jnp.int32),
            pltpu.SemaphoreType.DMA((4,)),
        ],
        name="prologue",
    )(where, trace, quadrature, gains[None], lags.T)
    chunks = jnp.broadcast_to(chunk[None], (SRC, STA, ROWS, 128)).reshape(DEV, ROWS, 128)
    received = lax.all_to_all(chunks, ("src", "sta"), 0, 0, tiled=True)

    def from_sta(x, k):
        return lax.ppermute(x, "sta", [((j + k) % STA, j) for j in range(STA)])

    middle = SRC // STEPS
    pairs = [(i + 1, i) for i in range(middle - 1)] + [(i - 1, i) for i in range(middle + 1, SRC)]
    edge = lax.ppermute(near, "src", pairs)
    edge = edge + lax.ppermute(far, "src", [(middle, middle - 1), (middle - 1, middle)])
    blocks = [own] + [from_sta(own, k) for k in range(1, STA)]
    edges = [edge] + [from_sta(edge, k) for k in range(1, STA)]
    win, gain = call(
        window,
        [shape((ROWS_IN, STATIONS)), shape((8, STATIONS))],
        [SMEM] + [VMEM] * 8,
        [pltpu.VMEM((STATIONS, 384), F32), pltpu.VMEM((STATIONS, 128), F32), pltpu.VMEM((512, STATIONS), F32)],
        name="window",
    )(where, *blocks, *edges)
    power = call(
        beams,
        shape((8, 128)),
        [SMEM] + [VMEM] * 3,
        [pltpu.VMEM((16, ROWS_OUT + 48, STATIONS), BF16), pltpu.VMEM((2, STATIONS, 512), BF16)],
        name="beams",
    )(where, received, win, gain)
    parts = lax.all_to_all(jnp.broadcast_to(power[None], (DEV, 8, 128)), ("src", "sta"), 0, 0, tiled=True)
    return call(finish, shape((STEPS, CPD)), [SMEM, VMEM], [pltpu.VMEM((32, 128), F32)], name="finish")(where, parts)


def solution(mesh):
    return jax.shard_map(
        on_device,
        mesh=mesh,
        in_specs=(P("sta", "src"), P("sta", "src"), P("sta"), P("src", "sta")),
        out_specs=P(None, "src"),
        check_vma=False,
    )
```

```python
import jax
import jax.numpy as jnp
from jax import lax
from jax.experimental import pallas as pl
from jax.experimental.pallas import tpu as pltpu
from jax.sharding import PartitionSpec as P


W = 4096
LAGS = 64
STEPS = 2
F32 = jnp.float32
BF16 = jnp.bfloat16
VMEM = pl.BlockSpec(memory_space=pltpu.VMEM)
SMEM = pl.BlockSpec(memory_space=pltpu.SMEM)

SRC = 32
STA = 4
DEV = SRC * STA
BLK = 258
ST = 64
STATIONS = ST * STA
HALO = LAGS - 1
CHAIN = 64
ROWS_OUT = 264
ROWS_IN = ROWS_OUT + LAGS
CPD = 128
ROWS = 24
SAMPLES = BLK * SRC
HALF = SRC // STEPS * STA


def prologue(where, trace, quad, gains, lags, own, chunk, tr_in, qd_in, ga_in, lg_in, sem):
    copies = [
        pltpu.make_async_copy(a, b, sem.at[k])
        for k, (a, b) in enumerate(((trace, tr_in), (quad, qd_in), (gains, ga_in), (lags, lg_in)))
    ]
    for copy in copies:
        copy.start()
    for copy in copies:
        copy.wait()
    tr, qd = tr_in[...], qd_in[...]
    energy = tr * tr + qd * qd
    own[:, :BLK] = energy
    gain = jnp.concatenate([ga_in[...], ga_in[...]], axis=1)
    gain = jnp.broadcast_to(gain, (128, 128)).T[:ST]
    own[:, BLK:] = gain[:, : 384 - BLK]
    total = jnp.sum(energy, axis=1, keepdims=True)
    total = jnp.broadcast_to(total, (ST, 128))
    total = jnp.concatenate([total, total], axis=0).T[:8]
    hi = total.astype(BF16).astype(F32)
    mid = (total - hi).astype(BF16).astype(F32)
    low = total - hi - mid
    row = lax.broadcasted_iota(jnp.int32, (8, 128), 0)
    lane = lax.broadcasted_iota(jnp.int32, (8, 128), 1)
    sums = jnp.where(row == 0, hi, jnp.where(row == 1, mid, jnp.where(row == 2, low, 0.0)))
    sums = jnp.where(lane // ST == where[1] % 2, sums, 0.0)
    lag = lg_in[...].astype(F32)
    lag = jnp.concatenate([lag, lag], axis=0).T
    for j in range(STA):
        body = jnp.where(lane[:1] < ST, lag[32 * j : 32 * j + 16], lag[32 * j + 16 : 32 * j + 32])
        chunk[j] = jnp.concatenate([body, sums], axis=0).astype(BF16)


def turn(where, e0, e1, e2, e3, main, near, far, tall):
    for k, e in enumerate((e0, e1, e2, e3)):
        at = pl.multiple_of((where[1] + k) % STA * ST, ST)
        tall[pl.ds(at, ST), :] = e[...]
    main[...] = tall[...].T
    first, last = main[0:64, :], main[BLK - 64 : BLK, :]
    low_half = where[0] < SRC // STEPS
    near[...] = jnp.where(low_half, first, last)
    far[...] = jnp.where(low_half, last, first)


def beams(where, received, main, halo, far_halo, power, line, weighted, lagged):
    halves = []
    for half in range(2):
        acc = jnp.zeros((8, 128), F32)
        for i in range(SRC):
            for j in (2 * half, 2 * half + 1):
                acc = acc + received[STA * i + j, 16:24, :].astype(F32)
        halves.append(jnp.sum(acc, axis=0, keepdims=True))
    baseline = jnp.concatenate(halves, axis=1) / SAMPLES
    gain = main[BLK : BLK + 1, :]

    def weigh(energy):
        return (gain * (energy - baseline)).astype(BF16).astype(F32)

    src = where[0]
    middle = SRC // STEPS
    edge = weigh(halo[...] + far_halo[...])

    @pl.when(src < middle)
    def _():
        line[0:264, :] = weigh(main[0:264, :])
        line[BLK : BLK + 64, :] = edge

    @pl.when(src >= middle)
    def _():
        line[0:HALO, :] = edge[1:64]
        line[HALO : HALO + 264, :] = weigh(main[0:264, :])

    for b in range(16):
        weighted[b] = line[b : b + ROWS_OUT + 48, :].astype(BF16)
    start = jnp.where(src == middle, W - (BLK * middle - HALO), 0)
    stop = jnp.where(src == middle - 1, W - BLK * (middle - 1), jnp.where(src == SRC - 1, BLK - 1, BLK))
    row = lax.broadcasted_iota(jnp.int32, (ROWS_OUT, 256), 0)
    inside = jnp.logical_and(row >= start, row < stop)
    for j in range(STA):
        part = jnp.concatenate([received[STA * i + j, 0:16, :] for i in range(SRC)], axis=0)
        part = part.astype(F32).T.astype(BF16)
        for group in range(4):
            lagged[group, ST * j : ST * j + ST, :] = part[
                ST * (group // 2) : ST * (group // 2) + ST, 256 * (group % 2) : 256 * (group % 2) + 256
            ]

    def one(group, carry):
        lag = lagged[group]

        def add(step, total):
            base = pl.multiple_of(step * CHAIN, 16)
            picks, shifted = [], []
            for b in range(CHAIN):
                value = (base + b).astype(F32).astype(BF16) if CHAIN < LAGS else BF16(b)
                picks.append(jnp.where(lag == value, BF16(1), BF16(0)))
                shifted.append(weighted[b % 16, pl.ds(base + b // 16 * 16, ROWS_OUT), :])
            return total + jnp.dot(
                jnp.concatenate(shifted, axis=1), jnp.concatenate(picks, axis=0), preferred_element_type=F32
            )

        if CHAIN < LAGS:
            beam = lax.fori_loop(0, LAGS // CHAIN, add, jnp.zeros((ROWS_OUT, 256), F32))
        else:
            beam = add(0, 0.0)
        beam = jnp.where(inside, beam, 0.0)
        squared = jnp.sum(beam * beam, axis=0, keepdims=True)
        power[group, 0] = squared[:, :128]
        power[group, 1] = squared[:, 128:]
        return carry

    lax.fori_loop(0, 4, one, 0)


def finish(where, parts, out, sums):
    src = where[0]
    lane = lax.broadcasted_iota(jnp.int32, (1, 128), 1)
    for k in range(STEPS):
        peak = None
        for j in range(STA):
            acc = parts[k * HALF + j]
            for i in range(1, SRC // STEPS):
                acc = acc + parts[k * HALF + STA * i + j]
            sums[8 * j : 8 * j + 8, :] = acc
            peak = acc if peak is None else jnp.maximum(peak, acc)
        peak = jnp.max(peak, axis=(0, 1), keepdims=True)
        cells = jnp.zeros((1, 128), F32)
        for j in range(STA):
            for h in range(2):
                row = sums[pl.ds(8 * j + 4 * h + src // 8, 1), :]
                to = 32 * j + 16 * h
                row = pltpu.roll(row, (to - 16 * (src % 8)) % 128, 1)
                cells = jnp.where(lane // 16 == to // 16, row, cells)
        out[k : k + 1, :] = cells / peak


def call(kernel, out_shape, specs, scratch=()):
    multi = isinstance(out_shape, (list, tuple))
    return pl.pallas_call(
        kernel,
        out_shape=out_shape,
        in_specs=specs,
        out_specs=[VMEM] * len(out_shape) if multi else VMEM,
        scratch_shapes=scratch,
        compiler_params=pltpu.CompilerParams(vmem_limit_bytes=48 << 20),
    )


def shape(dims, dtype=F32):
    return jax.ShapeDtypeStruct(dims, dtype)


def program(trace, quadrature, gains, lags):
    where = jnp.stack([lax.axis_index("src"), lax.axis_index("sta")]).astype(jnp.int32)
    inputs = [pltpu.with_memory_space_constraint(x, pltpu.HBM) for x in (trace, quadrature, gains[None], lags.T)]
    own, chunk = call(
        prologue,
        [shape((ST, 384)), shape((STA, ROWS, 128), BF16)],
        [SMEM] + [pl.BlockSpec(memory_space=pltpu.HBM)] * 4,
        [
            pltpu.VMEM((ST, BLK), F32),
            pltpu.VMEM((ST, BLK), F32),
            pltpu.VMEM((1, ST), F32),
            pltpu.VMEM((ST, CPD), jnp.int32),
            pltpu.SemaphoreType.DMA((4,)),
        ],
    )(where, *inputs)
    blocks = [own]
    for k in range(1, STA):
        blocks.append(lax.ppermute(own, "sta", [((j + k) % STA, j) for j in range(STA)]))
    chunks = jnp.broadcast_to(chunk[None], (SRC, STA, ROWS, 128)).reshape(DEV, ROWS, 128)
    received = lax.all_to_all(chunks, ("src", "sta"), 0, 0, tiled=True)
    main, near, far = call(
        turn,
        [shape((384, STATIONS)), shape((64, STATIONS)), shape((64, STATIONS))],
        [SMEM] + [VMEM] * 4,
        [pltpu.VMEM((STATIONS, 384), F32)],
    )(where, *blocks)
    middle = SRC // STEPS
    pairs = [(i + 1, i) for i in range(middle - 1)] + [(i - 1, i) for i in range(middle + 1, SRC)]
    halo = lax.ppermute(near, "src", pairs)
    far_halo = lax.ppermute(far, "src", [(middle, middle - 1), (middle - 1, middle)])
    power = call(
        beams,
        shape((4, 2, 1, 128)),
        [SMEM] + [VMEM] * 4,
        [
            pltpu.VMEM((ROWS_IN, STATIONS), F32),
            pltpu.VMEM((16, ROWS_OUT + 48, STATIONS), BF16),
            pltpu.VMEM((4, STATIONS, 256), BF16),
        ],
    )(where, received, main, halo, far_halo)
    power = power.reshape(8, 128)
    parts = lax.all_to_all(jnp.broadcast_to(power[None], (DEV, 8, 128)), ("src", "sta"), 0, 0, tiled=True)
    return call(finish, shape((STEPS, CPD)), [SMEM, VMEM], [pltpu.VMEM((32, 128), F32)])(where, parts)


def solution(mesh):
    return jax.shard_map(
        program,
        mesh=mesh,
        in_specs=(P("sta", "src"), P("sta", "src"), P("sta"), P("src", "sta")),
        out_specs=P(None, "src"),
        check_vma=False,
    )
```

```python
import jax
import jax.numpy as jnp
from jax import lax
from jax.experimental import pallas as pl
from jax.experimental.pallas import tpu as pltpu
from jax.sharding import PartitionSpec as P


W = 4096
LAGS = 64
STEPS = 2
F32 = jnp.float32
BF16 = jnp.bfloat16
VMEM = pl.BlockSpec(memory_space=pltpu.VMEM)

SRC = 32
STA = 4
DEV = SRC * STA
BLK = 258
ST = 64
STATIONS = ST * STA
HALO = LAGS - 1
CHAIN = 64
ROWS_OUT = 264
ROWS_IN = ROWS_OUT + LAGS
CPD = 128
ROWS = 24
SAMPLES = BLK * SRC
HALF = SRC // STEPS * STA


def prologue(trace, quad, gains, lags, own, chunk, tr_in, qd_in, ga_in, lg_in, sem):
    copies = [
        pltpu.make_async_copy(a, b, sem.at[k])
        for k, (a, b) in enumerate(((trace, tr_in), (quad, qd_in), (gains, ga_in), (lags, lg_in)))
    ]
    for copy in copies:
        copy.start()
    for copy in copies:
        copy.wait()
    tr, qd = tr_in[...], qd_in[...]
    energy = tr * tr + qd * qd
    own[:, :BLK] = energy
    gain = jnp.concatenate([ga_in[...], ga_in[...]], axis=1)
    gain = jnp.broadcast_to(gain, (128, 128)).T[:ST]
    own[:, BLK:] = gain[:, : 384 - BLK]
    total = jnp.sum(energy, axis=1, keepdims=True)
    total = jnp.broadcast_to(total, (ST, 128))
    total = jnp.concatenate([total, total], axis=0).T[:8]
    hi = total.astype(BF16).astype(F32)
    mid = (total - hi).astype(BF16).astype(F32)
    low = total - hi - mid
    row = lax.broadcasted_iota(jnp.int32, (8, 128), 0)
    lane = lax.broadcasted_iota(jnp.int32, (8, 128), 1)
    sums = jnp.where(row == 0, hi, jnp.where(row == 1, mid, jnp.where(row == 2, low, 0.0)))
    sums = jnp.where(lane // ST == lax.axis_index("sta") % 2, sums, 0.0)
    lag = lg_in[...].astype(F32)
    lag = jnp.concatenate([lag, lag], axis=0).T
    for j in range(STA):
        body = jnp.where(lane[:1] < ST, lag[32 * j : 32 * j + 16], lag[32 * j + 16 : 32 * j + 32])
        chunk[j] = jnp.concatenate([body, sums], axis=0).astype(BF16)


def turn(e0, e1, e2, e3, main, near, far, tall):
    for k, e in enumerate((e0, e1, e2, e3)):
        at = pl.multiple_of((lax.axis_index("sta") + k) % STA * ST, ST)
        tall[pl.ds(at, ST), :] = e[...]
    main[...] = tall[...].T
    first, last = main[0:64, :], main[BLK - 64 : BLK, :]
    low_half = lax.axis_index("src") < SRC // STEPS
    near[...] = jnp.where(low_half, first, last)
    far[...] = jnp.where(low_half, last, first)


def beams(received, main, halo, far_halo, power, line, weighted, lagged):
    halves = []
    for half in range(2):
        acc = jnp.zeros((8, 128), F32)
        for i in range(SRC):
            for j in (2 * half, 2 * half + 1):
                acc = acc + received[STA * i + j, 16:24, :].astype(F32)
        halves.append(jnp.sum(acc, axis=0, keepdims=True))
    baseline = jnp.concatenate(halves, axis=1) / SAMPLES
    gain = main[BLK : BLK + 1, :]

    def weigh(energy):
        return (gain * (energy - baseline)).astype(BF16).astype(F32)

    src = lax.axis_index("src")
    middle = SRC // STEPS
    edge = weigh(halo[...] + far_halo[...])

    @pl.when(src < middle)
    def _():
        line[0:264, :] = weigh(main[0:264, :])
        line[BLK : BLK + 64, :] = edge

    @pl.when(src >= middle)
    def _():
        line[0:HALO, :] = edge[1:64]
        line[HALO : HALO + 264, :] = weigh(main[0:264, :])

    for b in range(16):
        weighted[b] = line[b : b + ROWS_OUT + 48, :].astype(BF16)
    start = jnp.where(src == middle, W - (BLK * middle - HALO), 0)
    stop = jnp.where(src == middle - 1, W - BLK * (middle - 1), jnp.where(src == SRC - 1, BLK - 1, BLK))
    row = lax.broadcasted_iota(jnp.int32, (ROWS_OUT, 256), 0)
    inside = jnp.logical_and(row >= start, row < stop)
    for j in range(STA):
        part = jnp.concatenate([received[STA * i + j, 0:16, :] for i in range(SRC)], axis=0)
        part = part.astype(F32).T.astype(BF16)
        for group in range(4):
            lagged[group, ST * j : ST * j + ST, :] = part[
                ST * (group // 2) : ST * (group // 2) + ST, 256 * (group % 2) : 256 * (group % 2) + 256
            ]

    def one(group, carry):
        lag = lagged[group]

        def add(step, total):
            base = pl.multiple_of(step * CHAIN, 16)
            picks, shifted = [], []
            for b in range(CHAIN):
                value = (base + b).astype(F32).astype(BF16) if CHAIN < LAGS else BF16(b)
                picks.append(jnp.where(lag == value, BF16(1), BF16(0)))
                shifted.append(weighted[b % 16, pl.ds(base + b // 16 * 16, ROWS_OUT), :])
            return total + jnp.dot(
                jnp.concatenate(shifted, axis=1), jnp.concatenate(picks, axis=0), preferred_element_type=F32
            )

        if CHAIN < LAGS:
            beam = lax.fori_loop(0, LAGS // CHAIN, add, jnp.zeros((ROWS_OUT, 256), F32))
        else:
            beam = add(0, 0.0)
        beam = jnp.where(inside, beam, 0.0)
        squared = jnp.sum(beam * beam, axis=0, keepdims=True)
        power[group, 0] = squared[:, :128]
        power[group, 1] = squared[:, 128:]
        return carry

    lax.fori_loop(0, 4, one, 0)


def finish(parts, out, sums):
    src = lax.axis_index("src")
    lane = lax.broadcasted_iota(jnp.int32, (1, 128), 1)
    for k in range(STEPS):
        peak = None
        for j in range(STA):
            acc = parts[k * HALF + j]
            for i in range(1, SRC // STEPS):
                acc = acc + parts[k * HALF + STA * i + j]
            sums[8 * j : 8 * j + 8, :] = acc
            peak = acc if peak is None else jnp.maximum(peak, acc)
        peak = jnp.max(peak, axis=(0, 1), keepdims=True)
        cells = jnp.zeros((1, 128), F32)
        for j in range(STA):
            for h in range(2):
                row = sums[pl.ds(8 * j + 4 * h + src // 8, 1), :]
                to = 32 * j + 16 * h
                row = pltpu.roll(row, (to - 16 * (src % 8)) % 128, 1)
                cells = jnp.where(lane // 16 == to // 16, row, cells)
        out[k : k + 1, :] = cells / peak


def call(kernel, out_shape, specs, scratch=()):
    multi = isinstance(out_shape, (list, tuple))
    return pl.pallas_call(
        kernel,
        out_shape=out_shape,
        in_specs=specs,
        out_specs=[VMEM] * len(out_shape) if multi else VMEM,
        scratch_shapes=scratch,
        compiler_params=pltpu.CompilerParams(vmem_limit_bytes=48 << 20),
    )


def shape(dims, dtype=F32):
    return jax.ShapeDtypeStruct(dims, dtype)


def program(trace, quadrature, gains, lags):
    inputs = [pltpu.with_memory_space_constraint(x, pltpu.HBM) for x in (trace, quadrature, gains[None], lags.T)]
    own, chunk = call(
        prologue,
        [shape((ST, 384)), shape((STA, ROWS, 128), BF16)],
        [pl.BlockSpec(memory_space=pltpu.HBM)] * 4,
        [
            pltpu.VMEM((ST, BLK), F32),
            pltpu.VMEM((ST, BLK), F32),
            pltpu.VMEM((1, ST), F32),
            pltpu.VMEM((ST, CPD), jnp.int32),
            pltpu.SemaphoreType.DMA((4,)),
        ],
    )(*inputs)
    blocks = [own]
    for k in range(1, STA):
        blocks.append(lax.ppermute(own, "sta", [((j + k) % STA, j) for j in range(STA)]))
    chunks = jnp.broadcast_to(chunk[None], (SRC, STA, ROWS, 128)).reshape(DEV, ROWS, 128)
    received = lax.all_to_all(chunks, ("src", "sta"), 0, 0, tiled=True)
    main, near, far = call(
        turn,
        [shape((384, STATIONS)), shape((64, STATIONS)), shape((64, STATIONS))],
        [VMEM] * 4,
        [pltpu.VMEM((STATIONS, 384), F32)],
    )(*blocks)
    middle = SRC // STEPS
    pairs = [(i + 1, i) for i in range(middle - 1)] + [(i - 1, i) for i in range(middle + 1, SRC)]
    halo = lax.ppermute(near, "src", pairs)
    far_halo = lax.ppermute(far, "src", [(middle, middle - 1), (middle - 1, middle)])
    power = call(
        beams,
        shape((4, 2, 1, 128)),
        [VMEM] * 4,
        [
            pltpu.VMEM((ROWS_IN, STATIONS), F32),
            pltpu.VMEM((16, ROWS_OUT + 48, STATIONS), BF16),
            pltpu.VMEM((4, STATIONS, 256), BF16),
        ],
    )(received, main, halo, far_halo)
    power = power.reshape(8, 128)
    parts = lax.all_to_all(jnp.broadcast_to(power[None], (DEV, 8, 128)), ("src", "sta"), 0, 0, tiled=True)
    return call(finish, shape((STEPS, CPD)), [VMEM], [pltpu.VMEM((32, 128), F32)])(parts)


def solution(mesh):
    return jax.shard_map(
        program,
        mesh=mesh,
        in_specs=(P("sta", "src"), P("sta", "src"), P("sta"), P("src", "sta")),
        out_specs=P(None, "src"),
        check_vma=False,
    )
```

```python
import jax
import jax.numpy as jnp
from jax import lax
from jax.experimental import pallas as pl
from jax.experimental.pallas import tpu as pltpu
from jax.sharding import PartitionSpec as P


W = 4096
LAGS = 64
STEPS = 2
F32 = jnp.float32
BF16 = jnp.bfloat16
VMEM = pl.BlockSpec(memory_space=pltpu.VMEM)

SRC = 32
STA = 4
DEV = SRC * STA
BLK = 258
ST = 64
STATIONS = ST * STA
HALO = LAGS - 1
CHAIN = 64
ROWS_OUT = 264
ROWS_IN = ROWS_OUT + LAGS
CPD = 128
WIDE = 9 * 128
SAMPLES = BLK * SRC
HALF = SRC // STEPS * STA


def prologue(trace, quad, gains, lags, own, chunk, tr_in, qd_in, ga_in, lg_in, sem):
    copies = [
        pltpu.make_async_copy(a, b, sem.at[k])
        for k, (a, b) in enumerate(((trace, tr_in), (quad, qd_in), (gains, ga_in), (lags, lg_in)))
    ]
    for copy in copies:
        copy.start()
    for copy in copies:
        copy.wait()
    tr, qd = tr_in[...], qd_in[...]
    energy = tr * tr + qd * qd
    own[:, :BLK] = energy
    gain = jnp.concatenate([ga_in[...], ga_in[...]], axis=1)
    gain = jnp.broadcast_to(gain, (128, 128)).T[:ST]
    own[:, BLK:] = gain[:, : 384 - BLK]
    total = jnp.sum(energy, axis=1, keepdims=True)
    total = jnp.broadcast_to(total, (ST, 128))
    total = jnp.concatenate([total, total], axis=0).T[:2]
    hi = total.astype(BF16).astype(F32)
    mid = (total - hi).astype(BF16).astype(F32)
    low = total - hi - mid
    row = lax.broadcasted_iota(jnp.int32, (2, 128), 0)
    lane = lax.broadcasted_iota(jnp.int32, (2, 128), 1)
    sums = jnp.where(row == 0, jnp.where(lane < ST, hi, mid), jnp.where(lane < ST, low, 0.0))
    lag = lg_in[...].astype(F32)
    lag = jnp.concatenate([lag, lag], axis=0).T
    for j in range(STA):
        body = jnp.where(lane[:1] < ST, lag[32 * j : 32 * j + 16], lag[32 * j + 16 : 32 * j + 32])
        pieces = [body[2 * k : 2 * k + 2] for k in range(8)] + [sums]
        chunk[j] = jnp.concatenate(pieces, axis=1).astype(BF16)


def turn(e0, e1, e2, e3, main, near, far, tall):
    for k, e in enumerate((e0, e1, e2, e3)):
        at = pl.multiple_of((lax.axis_index("sta") + k) % STA * ST, ST)
        tall[pl.ds(at, ST), :] = e[...]
    main[...] = tall[...].T
    first, last = main[0:64, :], main[BLK - 64 : BLK, :]
    low_half = lax.axis_index("src") < SRC // STEPS
    near[...] = jnp.where(low_half, first, last)
    far[...] = jnp.where(low_half, last, first)


def beams(received, main, halo, far_halo, power, line, weighted, lagged, opened):
    lane = lax.broadcasted_iota(jnp.int32, (1, 128), 1)
    totals = []
    for j in range(STA):
        acc = jnp.zeros((2, 128), F32)
        for i in range(SRC):
            acc = acc + received[STA * i + j, :, 1024:].astype(F32)
        acc = acc[0:1] + acc[1:2]
        totals.append(acc + pltpu.roll(acc, ST, 1))
    halves = [jnp.where(lane < ST, totals[0], totals[1]), jnp.where(lane < ST, totals[2], totals[3])]
    baseline = jnp.concatenate(halves, axis=1) / SAMPLES
    gain = main[BLK : BLK + 1, :]

    def weigh(energy):
        return (gain * (energy - baseline)).astype(BF16).astype(F32)

    src = lax.axis_index("src")
    middle = SRC // STEPS
    edge = weigh(halo[...] + far_halo[...])

    @pl.when(src < middle)
    def _():
        line[0:264, :] = weigh(main[0:264, :])
        line[BLK : BLK + 64, :] = edge

    @pl.when(src >= middle)
    def _():
        line[0:HALO, :] = edge[1:64]
        line[HALO : HALO + 264, :] = weigh(main[0:264, :])

    for b in range(16):
        weighted[b] = line[b : b + ROWS_OUT + 48, :].astype(BF16)
    start = jnp.where(src == middle, W - (BLK * middle - HALO), 0)
    stop = jnp.where(src == middle - 1, W - BLK * (middle - 1), jnp.where(src == SRC - 1, BLK - 1, BLK))
    row = lax.broadcasted_iota(jnp.int32, (ROWS_OUT, 256), 0)
    inside = jnp.logical_and(row >= start, row < stop)
    for j in range(STA):
        for i in range(SRC):
            for k in range(8):
                opened[16 * i + 2 * k : 16 * i + 2 * k + 2, :] = received[
                    STA * i + j, :, 128 * k : 128 * k + 128
                ].astype(F32)
        part = opened[...].T.astype(BF16)
        for group in range(4):
            lagged[group, ST * j : ST * j + ST, :] = part[
                ST * (group // 2) : ST * (group // 2) + ST, 256 * (group % 2) : 256 * (group % 2) + 256
            ]

    def one(group, carry):
        lag = lagged[group]

        def add(step, total):
            base = pl.multiple_of(step * CHAIN, 16)
            picks, shifted = [], []
            for b in range(CHAIN):
                value = (base + b).astype(F32).astype(BF16) if CHAIN < LAGS else BF16(b)
                picks.append(jnp.where(lag == value, BF16(1), BF16(0)))
                shifted.append(weighted[b % 16, pl.ds(base + b // 16 * 16, ROWS_OUT), :])
            return total + jnp.dot(
                jnp.concatenate(shifted, axis=1), jnp.concatenate(picks, axis=0), preferred_element_type=F32
            )

        if CHAIN < LAGS:
            beam = lax.fori_loop(0, LAGS // CHAIN, add, jnp.zeros((ROWS_OUT, 256), F32))
        else:
            beam = add(0, 0.0)
        beam = jnp.where(inside, beam, 0.0)
        squared = jnp.sum(beam * beam, axis=0, keepdims=True)
        power[group, 0] = squared[:, :128]
        power[group, 1] = squared[:, 128:]
        return carry

    lax.fori_loop(0, 4, one, 0)


def finish(parts, out, sums):
    src = lax.axis_index("src")
    lane = lax.broadcasted_iota(jnp.int32, (1, 128), 1)
    for k in range(STEPS):
        peak = None
        for j in range(STA):
            acc = parts[k * HALF + j]
            for i in range(1, SRC // STEPS):
                acc = acc + parts[k * HALF + STA * i + j]
            sums[8 * j : 8 * j + 8, :] = acc
            peak = acc if peak is None else jnp.maximum(peak, acc)
        peak = jnp.max(peak, axis=(0, 1), keepdims=True)
        cells = jnp.zeros((1, 128), F32)
        for j in range(STA):
            for h in range(2):
                row = sums[pl.ds(8 * j + 4 * h + src // 8, 1), :]
                to = 32 * j + 16 * h
                row = pltpu.roll(row, (to - 16 * (src % 8)) % 128, 1)
                cells = jnp.where(lane // 16 == to // 16, row, cells)
        out[k : k + 1, :] = cells / peak


def call(kernel, out_shape, specs, scratch=()):
    multi = isinstance(out_shape, (list, tuple))
    return pl.pallas_call(
        kernel,
        out_shape=out_shape,
        in_specs=specs,
        out_specs=[VMEM] * len(out_shape) if multi else VMEM,
        scratch_shapes=scratch,
        compiler_params=pltpu.CompilerParams(vmem_limit_bytes=48 << 20),
    )


def shape(dims, dtype=F32):
    return jax.ShapeDtypeStruct(dims, dtype)


def program(trace, quadrature, gains, lags):
    inputs = [pltpu.with_memory_space_constraint(x, pltpu.HBM) for x in (trace, quadrature, gains[None], lags.T)]
    own, chunk = call(
        prologue,
        [shape((ST, 384)), shape((STA, 2, WIDE), BF16)],
        [pl.BlockSpec(memory_space=pltpu.HBM)] * 4,
        [
            pltpu.VMEM((ST, BLK), F32),
            pltpu.VMEM((ST, BLK), F32),
            pltpu.VMEM((1, ST), F32),
            pltpu.VMEM((ST, CPD), jnp.int32),
            pltpu.SemaphoreType.DMA((4,)),
        ],
    )(*inputs)
    blocks = [own]
    for k in range(1, STA):
        blocks.append(lax.ppermute(own, "sta", [((j + k) % STA, j) for j in range(STA)]))
    chunks = jnp.broadcast_to(chunk[None], (SRC, STA, 2, WIDE)).reshape(DEV, 2, WIDE)
    received = lax.all_to_all(chunks, ("src", "sta"), 0, 0, tiled=True)
    main, near, far = call(
        turn,
        [shape((384, STATIONS)), shape((64, STATIONS)), shape((64, STATIONS))],
        [VMEM] * 4,
        [pltpu.VMEM((STATIONS, 384), F32)],
    )(*blocks)
    middle = SRC // STEPS
    pairs = [(i + 1, i) for i in range(middle - 1)] + [(i - 1, i) for i in range(middle + 1, SRC)]
    halo = lax.ppermute(near, "src", pairs)
    far_halo = lax.ppermute(far, "src", [(middle, middle - 1), (middle - 1, middle)])
    power = call(
        beams,
        shape((4, 2, 1, 128)),
        [VMEM] * 4,
        [
            pltpu.VMEM((ROWS_IN, STATIONS), F32),
            pltpu.VMEM((16, ROWS_OUT + 48, STATIONS), BF16),
            pltpu.VMEM((4, STATIONS, 256), BF16),
            pltpu.VMEM((512, 128), F32),
        ],
    )(received, main, halo, far_halo)
    power = power.reshape(8, 128)
    parts = lax.all_to_all(jnp.broadcast_to(power[None], (DEV, 8, 128)), ("src", "sta"), 0, 0, tiled=True)
    return call(finish, shape((STEPS, CPD)), [VMEM], [pltpu.VMEM((32, 128), F32)])(parts)


def solution(mesh):
    return jax.shard_map(
        program,
        mesh=mesh,
        in_specs=(P("sta", "src"), P("sta", "src"), P("sta"), P("src", "sta")),
        out_specs=P(None, "src"),
        check_vma=False,
    )
```

```python
import jax
import jax.numpy as jnp
from jax import lax
from jax.experimental import pallas as pl
from jax.experimental.pallas import tpu as pltpu
from jax.sharding import PartitionSpec as P


W = 4096
LAGS = 64
STEPS = 2
F32 = jnp.float32
BF16 = jnp.bfloat16
VMEM = pl.BlockSpec(memory_space=pltpu.VMEM)

SRC = 32
STA = 4
DEV = SRC * STA
BLK = 258
ST = 64
STATIONS = ST * STA
HALO = LAGS - 1
COPIES = 16
CPD = 128
WIDE = 9 * 128
SAMPLES = BLK * SRC
HALF = SRC // STEPS * STA


def prologue(trace, quad, gains, lags, own, chunk, tr_in, qd_in, ga_in, lg_in, sem):
    copies = [
        pltpu.make_async_copy(a, b, sem.at[k])
        for k, (a, b) in enumerate(((trace, tr_in), (quad, qd_in), (gains, ga_in), (lags, lg_in)))
    ]
    for copy in copies:
        copy.start()
    for copy in copies:
        copy.wait()
    tr, qd = tr_in[...], qd_in[...]
    energy = tr * tr + qd * qd
    own[:, :BLK] = energy
    gain = jnp.concatenate([ga_in[...], ga_in[...]], axis=1)
    gain = jnp.broadcast_to(gain, (128, 128)).T[:ST]
    own[:, BLK:] = gain[:, : 384 - BLK]
    total = jnp.sum(energy, axis=1, keepdims=True)
    total = jnp.broadcast_to(total, (ST, 128))
    total = jnp.concatenate([total, total], axis=0).T[:2]
    hi = total.astype(BF16).astype(F32)
    mid = (total - hi).astype(BF16).astype(F32)
    low = total - hi - mid
    row = lax.broadcasted_iota(jnp.int32, (2, 128), 0)
    lane = lax.broadcasted_iota(jnp.int32, (2, 128), 1)
    sums = jnp.where(row == 0, jnp.where(lane < ST, hi, mid), jnp.where(lane < ST, low, 0.0))
    lag = lg_in[...].astype(F32)
    lag = jnp.concatenate([lag, lag], axis=0).T
    for j in range(STA):
        body = jnp.where(lane[:1] < ST, lag[32 * j : 32 * j + 16], lag[32 * j + 16 : 32 * j + 32])
        pieces = [body[2 * k : 2 * k + 2] for k in range(8)] + [sums]
        chunk[j] = jnp.concatenate(pieces, axis=1).astype(BF16)


def turn(e0, e1, e2, e3, main, near, far, tall):
    for k, e in enumerate((e0, e1, e2, e3)):
        at = pl.multiple_of((lax.axis_index("sta") + k) % STA * ST, ST)
        tall[pl.ds(at, ST), :] = e[...]
    main[...] = tall[...].T
    first, last = main[0:64, :], main[BLK - 64 : BLK, :]
    low_half = lax.axis_index("src") < SRC // STEPS
    near[...] = jnp.where(low_half, first, last)
    far[...] = jnp.where(low_half, last, first)


def beams(received, main, halo, far_halo, power, line, weighted, table, lagged, opened):
    src = lax.axis_index("src")
    middle = SRC // STEPS
    lane = lax.broadcasted_iota(jnp.int32, (1, 128), 1)
    left = lane < ST
    totals = []
    for j in range(STA):
        acc = jnp.zeros((2, 128), F32)
        for i in range(SRC):
            acc = acc + received[STA * i + j, :, 1024:].astype(F32)
        acc = acc[0:1] + acc[1:2]
        totals.append(acc + pltpu.roll(acc, ST, 1))
    halves = [jnp.where(left, totals[0], totals[1]), jnp.where(left, totals[2], totals[3])]
    baseline = jnp.concatenate(halves, axis=1) / SAMPLES
    gain = main[BLK : BLK + 1, :]

    def weigh(energy):
        return (gain * (energy - baseline)).astype(BF16).astype(F32)

    edge = weigh(halo[...] + far_halo[...])

    @pl.when(src < middle)
    def _():
        line[0:264, :] = weigh(main[0:264, :])
        line[BLK : BLK + 64, :] = edge

    @pl.when(src >= middle)
    def _():
        line[0:HALO, :] = edge[1:64]
        line[HALO : HALO + 264, :] = weigh(main[0:264, :])

    for b in range(COPIES):
        weighted[b] = line[b : b + 256 + LAGS - COPIES, :].astype(BF16)
    table[...] = line[256:384, :].T
    extra = [[jnp.zeros((8, 512), F32) for _ in range(2)] for _ in range(2)]
    for j in range(STA):
        for i in range(SRC):
            for k in range(8):
                opened[j, 16 * i + 2 * k : 16 * i + 2 * k + 2, :] = received[
                    STA * i + j, :, 128 * k : 128 * k + 128
                ].astype(F32)
        part = opened[j].T.astype(jnp.int32)
        for h in range(2):
            for row in range(0, ST, 8):
                entry = table[ST * j + row : ST * j + row + 8, :]
                index = part[ST * h + row : ST * h + row + 8]
                for k in range(2):
                    found = [
                        jnp.take_along_axis(entry, index[:, c : c + 128] + k, axis=1, mode="promise_in_bounds")
                        for c in range(0, 512, 128)
                    ]
                    extra[h][k] = extra[h][k] + jnp.concatenate(found, axis=1)
    for t in range(2):
        one, two = opened[2 * t], opened[2 * t + 1]
        lagged[0:512, 128 * t : 128 * t + 128] = jnp.where(left, one, pltpu.roll(two, ST, 1)).astype(BF16)
        lagged[512:, 128 * t : 128 * t + 128] = jnp.where(left, pltpu.roll(one, ST, 1), two).astype(BF16)
    start = jnp.where(src == middle, W - (BLK * middle - HALO), 0)
    stop = jnp.where(src == middle - 1, W - BLK * (middle - 1), jnp.where(src == SRC - 1, BLK - 1, BLK))
    at = lax.broadcasted_iota(jnp.int32, (1, 256), 1)
    inside = jnp.logical_and(at >= start, at < stop)
    lag = lagged[...]
    picks = [jnp.where(lag == BF16(b), BF16(1), BF16(0)) for b in range(LAGS)]
    shifted = [weighted[b % COPIES, b - b % COPIES : b - b % COPIES + 256, :] for b in range(LAGS)]
    beam = lax.dot_general(
        jnp.concatenate(picks, axis=1),
        jnp.concatenate(shifted, axis=1),
        (((1,), (1,)), ((), ())),
        preferred_element_type=F32,
    )
    beam = jnp.where(inside, beam, 0.0)
    squared = beam * beam
    squared = jnp.sum((squared[:, :128] + squared[:, 128:]).T, axis=0, keepdims=True)
    for h in range(2):
        row = squared[:, 512 * h : 512 * h + 512]
        for k in range(2):
            late = jnp.sum(extra[h][k], axis=0, keepdims=True)
            row = row + jnp.where(256 + k < stop, late * late, 0.0)
        for g in range(4):
            power[4 * h + g : 4 * h + g + 1, :] = row[:, 128 * g : 128 * g + 128]


def finish(parts, out, sums):
    src = lax.axis_index("src")
    lane = lax.broadcasted_iota(jnp.int32, (1, 128), 1)
    for k in range(STEPS):
        peak = None
        for j in range(STA):
            acc = parts[k * HALF + j]
            for i in range(1, SRC // STEPS):
                acc = acc + parts[k * HALF + STA * i + j]
            sums[8 * j : 8 * j + 8, :] = acc
            peak = acc if peak is None else jnp.maximum(peak, acc)
        peak = jnp.max(peak, axis=(0, 1), keepdims=True)
        cells = jnp.zeros((1, 128), F32)
        for j in range(STA):
            for h in range(2):
                row = sums[pl.ds(8 * j + 4 * h + src // 8, 1), :]
                to = 32 * j + 16 * h
                row = pltpu.roll(row, (to - 16 * (src % 8)) % 128, 1)
                cells = jnp.where(lane // 16 == to // 16, row, cells)
        out[k : k + 1, :] = cells / peak


def call(kernel, out_shape, specs, scratch=()):
    multi = isinstance(out_shape, (list, tuple))
    return pl.pallas_call(
        kernel,
        out_shape=out_shape,
        in_specs=specs,
        out_specs=[VMEM] * len(out_shape) if multi else VMEM,
        scratch_shapes=scratch,
        compiler_params=pltpu.CompilerParams(vmem_limit_bytes=48 << 20),
    )


def shape(dims, dtype=F32):
    return jax.ShapeDtypeStruct(dims, dtype)


def program(trace, quadrature, gains, lags):
    inputs = [pltpu.with_memory_space_constraint(x, pltpu.HBM) for x in (trace, quadrature, gains[None], lags.T)]
    own, chunk = call(
        prologue,
        [shape((ST, 384)), shape((STA, 2, WIDE), BF16)],
        [pl.BlockSpec(memory_space=pltpu.HBM)] * 4,
        [
            pltpu.VMEM((ST, BLK), F32),
            pltpu.VMEM((ST, BLK), F32),
            pltpu.VMEM((1, ST), F32),
            pltpu.VMEM((ST, CPD), jnp.int32),
            pltpu.SemaphoreType.DMA((4,)),
        ],
    )(*inputs)
    blocks = [own]
    for k in range(1, STA):
        blocks.append(lax.ppermute(own, "sta", [((j + k) % STA, j) for j in range(STA)]))
    chunks = jnp.broadcast_to(chunk[None], (SRC, STA, 2, WIDE)).reshape(DEV, 2, WIDE)
    received = lax.all_to_all(chunks, ("src", "sta"), 0, 0, tiled=True)
    main, near, far = call(
        turn,
        [shape((384, STATIONS)), shape((64, STATIONS)), shape((64, STATIONS))],
        [VMEM] * 4,
        [pltpu.VMEM((STATIONS, 384), F32)],
    )(*blocks)
    middle = SRC // STEPS
    pairs = [(i + 1, i) for i in range(middle - 1)] + [(i - 1, i) for i in range(middle + 1, SRC)]
    halo = lax.ppermute(near, "src", pairs)
    far_halo = lax.ppermute(far, "src", [(middle, middle - 1), (middle - 1, middle)])
    power = call(
        beams,
        shape((8, 128)),
        [VMEM] * 4,
        [
            pltpu.VMEM((384, STATIONS), F32),
            pltpu.VMEM((COPIES, 256 + LAGS - COPIES, STATIONS), BF16),
            pltpu.VMEM((STATIONS, 128), F32),
            pltpu.VMEM((1024, STATIONS), BF16),
            pltpu.VMEM((STA, 512, 128), F32),
        ],
    )(received, main, halo, far_halo)
    parts = lax.all_to_all(jnp.broadcast_to(power[None], (DEV, 8, 128)), ("src", "sta"), 0, 0, tiled=True)
    return call(finish, shape((STEPS, CPD)), [VMEM], [pltpu.VMEM((32, 128), F32)])(parts)


def solution(mesh):
    return jax.shard_map(
        program,
        mesh=mesh,
        in_specs=(P("sta", "src"), P("sta", "src"), P("sta"), P("src", "sta")),
        out_specs=P(None, "src"),
        check_vma=False,
    )
```

```python
import jax
import jax.numpy as jnp
from jax import lax
from jax.experimental import pallas as pl
from jax.experimental.pallas import tpu as pltpu
from jax.sharding import PartitionSpec as P


W = 4096
LAGS = 64
STEPS = 2
F32 = jnp.float32
BF16 = jnp.bfloat16
VMEM = pl.BlockSpec(memory_space=pltpu.VMEM)

SRC = 32
STA = 4
DEV = SRC * STA
BLK = 258
ST = 64
STATIONS = ST * STA
HALO = LAGS - 1
COPIES = 16
CPD = 128
WIDE = 9 * 128
SAMPLES = BLK * SRC
HALF = SRC // STEPS * STA


def prologue(trace, quad, gains, lags, own, chunk, tr_in, qd_in, ga_in, lg_in, sem):
    copies = [
        pltpu.make_async_copy(a, b, sem.at[k])
        for k, (a, b) in enumerate(((trace, tr_in), (quad, qd_in), (gains, ga_in), (lags, lg_in)))
    ]
    for copy in copies:
        copy.start()
    for copy in copies:
        copy.wait()
    tr, qd = tr_in[...], qd_in[...]
    energy = tr * tr + qd * qd
    own[:, :BLK] = energy
    gain = jnp.concatenate([ga_in[...], ga_in[...]], axis=1)
    gain = jnp.broadcast_to(gain, (128, 128)).T[:ST]
    own[:, BLK:] = gain[:, : 384 - BLK]
    total = jnp.sum(energy, axis=1, keepdims=True)
    total = jnp.broadcast_to(total, (ST, 128))
    total = jnp.concatenate([total, total], axis=0).T[:2]
    hi = total.astype(BF16).astype(F32)
    mid = (total - hi).astype(BF16).astype(F32)
    low = total - hi - mid
    row = lax.broadcasted_iota(jnp.int32, (2, 128), 0)
    lane = lax.broadcasted_iota(jnp.int32, (2, 128), 1)
    sums = jnp.where(row == 0, jnp.where(lane < ST, hi, mid), jnp.where(lane < ST, low, 0.0))
    lag = lg_in[...].astype(F32)
    lag = jnp.concatenate([lag, lag], axis=0).T
    for j in range(STA):
        body = jnp.where(lane[:1] < ST, lag[32 * j : 32 * j + 16], lag[32 * j + 16 : 32 * j + 32])
        pieces = [body[2 * k : 2 * k + 2] for k in range(8)] + [sums]
        chunk[j] = jnp.concatenate(pieces, axis=1).astype(BF16)


def turn(e0, e1, e2, e3, main, near, far, tall):
    for k, e in enumerate((e0, e1, e2, e3)):
        at = pl.multiple_of((lax.axis_index("sta") ^ k) * ST, ST)
        tall[pl.ds(at, ST), :] = e[...]
    main[...] = tall[...].T
    first, last = main[0:64, :], main[BLK - 64 : BLK, :]
    low_half = lax.axis_index("src") < SRC // STEPS
    near[...] = jnp.where(low_half, first, last)
    far[...] = jnp.where(low_half, last, first)


def beams(received, main, halo, far_halo, power, line, weighted, table, lagged, opened):
    src = lax.axis_index("src")
    middle = SRC // STEPS
    lane = lax.broadcasted_iota(jnp.int32, (1, 128), 1)
    left = lane < ST
    totals = []
    for j in range(STA):
        acc = jnp.zeros((2, 128), F32)
        for i in range(SRC):
            acc = acc + received[STA * i + j, :, 1024:].astype(F32)
        acc = acc[0:1] + acc[1:2]
        totals.append(acc + pltpu.roll(acc, ST, 1))
    halves = [jnp.where(left, totals[0], totals[1]), jnp.where(left, totals[2], totals[3])]
    baseline = jnp.concatenate(halves, axis=1) / SAMPLES
    gain = main[BLK : BLK + 1, :]

    def weigh(energy):
        return (gain * (energy - baseline)).astype(BF16).astype(F32)

    edge = weigh(halo[...] + far_halo[...])

    @pl.when(src < middle)
    def _():
        line[0:264, :] = weigh(main[0:264, :])
        line[BLK : BLK + 64, :] = edge

    @pl.when(src >= middle)
    def _():
        line[0:HALO, :] = edge[1:64]
        line[HALO : HALO + 264, :] = weigh(main[0:264, :])

    for b in range(COPIES):
        weighted[b] = line[b : b + 256 + LAGS - COPIES, :].astype(BF16)
    table[...] = line[256:384, :].T
    extra = [[jnp.zeros((8, 512), F32) for _ in range(2)] for _ in range(2)]
    for j in range(STA):
        for i in range(SRC):
            for k in range(8):
                opened[j, 16 * i + 2 * k : 16 * i + 2 * k + 2, :] = received[
                    STA * i + j, :, 128 * k : 128 * k + 128
                ].astype(F32)
        part = opened[j].T.astype(jnp.int32)
        for h in range(2):
            for row in range(0, ST, 8):
                entry = table[ST * j + row : ST * j + row + 8, :]
                index = part[ST * h + row : ST * h + row + 8]
                for k in range(2):
                    found = [
                        jnp.take_along_axis(entry, index[:, c : c + 128] + k, axis=1, mode="promise_in_bounds")
                        for c in range(0, 512, 128)
                    ]
                    extra[h][k] = extra[h][k] + jnp.concatenate(found, axis=1)
    for t in range(2):
        one, two = opened[2 * t], opened[2 * t + 1]
        lagged[0:512, 128 * t : 128 * t + 128] = jnp.where(left, one, pltpu.roll(two, ST, 1)).astype(BF16)
        lagged[512:, 128 * t : 128 * t + 128] = jnp.where(left, pltpu.roll(one, ST, 1), two).astype(BF16)
    start = jnp.where(src == middle, W - (BLK * middle - HALO), 0)
    stop = jnp.where(src == middle - 1, W - BLK * (middle - 1), jnp.where(src == SRC - 1, BLK - 1, BLK))
    at = lax.broadcasted_iota(jnp.int32, (1, 256), 1)
    inside = jnp.logical_and(at >= start, at < stop)
    lag = lagged[...]
    picks = [jnp.where(lag == BF16(b), BF16(1), BF16(0)) for b in range(LAGS)]
    shifted = [weighted[b % COPIES, b - b % COPIES : b - b % COPIES + 256, :] for b in range(LAGS)]
    beam = lax.dot_general(
        jnp.concatenate(picks, axis=1),
        jnp.concatenate(shifted, axis=1),
        (((1,), (1,)), ((), ())),
        preferred_element_type=F32,
    )
    beam = jnp.where(inside, beam, 0.0)
    squared = beam * beam
    squared = jnp.sum((squared[:, :128] + squared[:, 128:]).T, axis=0, keepdims=True)
    for h in range(2):
        row = squared[:, 512 * h : 512 * h + 512]
        for k in range(2):
            late = jnp.sum(extra[h][k], axis=0, keepdims=True)
            row = row + jnp.where(256 + k < stop, late * late, 0.0)
        for g in range(4):
            power[4 * h + g : 4 * h + g + 1, :] = row[:, 128 * g : 128 * g + 128]


def finish(parts, out, sums):
    src = lax.axis_index("src")
    h = lax.axis_index("sta") % 2
    lane = lax.broadcasted_iota(jnp.int32, (1, 128), 1)
    for k in range(STEPS):
        peak = None
        for j in range(STA):
            acc = parts[k * HALF + j]
            for i in range(1, SRC // STEPS):
                acc = acc + parts[k * HALF + STA * i + j]
            sums[8 * j : 8 * j + 4, :] = acc
            peak = acc if peak is None else jnp.maximum(peak, acc)
        peak = jnp.max(peak, axis=(0, 1), keepdims=True)
        cells = jnp.zeros((1, 128), F32)
        for j in range(STA):
            row = sums[pl.ds(8 * j + src // 8, 1), :]
            to = 32 * j + 16 * h
            row = pltpu.roll(row, (to - 16 * (src % 8) + 128) % 128, 1)
            cells = jnp.where(lane // 16 == 2 * j + h, row, cells)
        out[k : k + 1, :] = cells
        out[STEPS + k : STEPS + k + 1, :] = jnp.broadcast_to(peak, (1, 128))


def call(kernel, out_shape, specs, scratch=()):
    multi = isinstance(out_shape, (list, tuple))
    return pl.pallas_call(
        kernel,
        out_shape=out_shape,
        in_specs=specs,
        out_specs=[VMEM] * len(out_shape) if multi else VMEM,
        scratch_shapes=scratch,
        compiler_params=pltpu.CompilerParams(vmem_limit_bytes=48 << 20),
    )


def shape(dims, dtype=F32):
    return jax.ShapeDtypeStruct(dims, dtype)


def program(trace, quadrature, gains, lags):
    inputs = [pltpu.with_memory_space_constraint(x, pltpu.HBM) for x in (trace, quadrature, gains[None], lags.T)]
    own, chunk = call(
        prologue,
        [shape((ST, 384)), shape((STA, 2, WIDE), BF16)],
        [pl.BlockSpec(memory_space=pltpu.HBM)] * 4,
        [
            pltpu.VMEM((ST, BLK), F32),
            pltpu.VMEM((ST, BLK), F32),
            pltpu.VMEM((1, ST), F32),
            pltpu.VMEM((ST, CPD), jnp.int32),
            pltpu.SemaphoreType.DMA((4,)),
        ],
    )(*inputs)
    blocks = [own]
    for k in range(1, STA):
        blocks.append(lax.ppermute(own, "sta", [(j ^ k, j) for j in range(STA)]))
    chunks = jnp.broadcast_to(chunk[None], (SRC, STA, 2, WIDE)).reshape(DEV, 2, WIDE)
    received = lax.all_to_all(chunks, ("src", "sta"), 0, 0, tiled=True)
    main, near, far = call(
        turn,
        [shape((384, STATIONS)), shape((64, STATIONS)), shape((64, STATIONS))],
        [VMEM] * 4,
        [pltpu.VMEM((STATIONS, 384), F32)],
    )(*blocks)
    middle = SRC // STEPS
    pairs = [(i + 1, i) for i in range(middle - 1)] + [(i - 1, i) for i in range(middle + 1, SRC)]
    halo = lax.ppermute(near, "src", pairs)
    far_halo = lax.ppermute(far, "src", [(middle, middle - 1), (middle - 1, middle)])
    power = call(
        beams,
        shape((8, 128)),
        [VMEM] * 4,
        [
            pltpu.VMEM((384, STATIONS), F32),
            pltpu.VMEM((COPIES, 256 + LAGS - COPIES, STATIONS), BF16),
            pltpu.VMEM((STATIONS, 128), F32),
            pltpu.VMEM((1024, STATIONS), BF16),
            pltpu.VMEM((STA, 512, 128), F32),
        ],
    )(received, main, halo, far_halo)
    halves = jnp.broadcast_to(power.reshape(1, 2, 4, 128), (DEV // 2, 2, 4, 128)).reshape(DEV, 4, 128)
    parts = lax.all_to_all(halves, ("src", "sta"), 0, 0, tiled=True)
    mine = call(finish, shape((2 * STEPS, CPD)), [VMEM], [pltpu.VMEM((32, 128), F32)])(parts)
    other = lax.ppermute(mine, "sta", [(0, 1), (1, 0), (2, 3), (3, 2)])
    cells = mine[:STEPS] + other[:STEPS]
    return cells / jnp.maximum(mine[STEPS:], other[STEPS:])


def solution(mesh):
    return jax.shard_map(
        program,
        mesh=mesh,
        in_specs=(P("sta", "src"), P("sta", "src"), P("sta"), P("src", "sta")),
        out_specs=P(None, "src"),
        check_vma=False,
    )
```

```python
import jax
import jax.numpy as jnp
from jax import lax
from jax.experimental import pallas as pl
from jax.experimental.pallas import tpu as pltpu
from jax.sharding import PartitionSpec as P


W = 4096
LAGS = 64
STEPS = 2
F32 = jnp.float32
BF16 = jnp.bfloat16
VMEM = pl.BlockSpec(memory_space=pltpu.VMEM)

SRC = 32
STA = 4
DEV = SRC * STA
BLK = 258
ST = 64
STATIONS = ST * STA
HALO = LAGS - 1
COPIES = 8
CPD = 128
WIDE = 9 * 128
SAMPLES = BLK * SRC
HALF = SRC // STEPS * STA


def prologue(trace, quad, gains, lags, own, chunk, tr_in, qd_in, ga_in, lg_in, sem):
    copies = [
        pltpu.make_async_copy(a, b, sem.at[k])
        for k, (a, b) in enumerate(((trace, tr_in), (quad, qd_in), (gains, ga_in), (lags, lg_in)))
    ]
    for copy in copies:
        copy.start()
    copies[3].wait()
    lag = lg_in[...].astype(F32)
    lag = jnp.concatenate([lag, lag], axis=0).T
    for copy in copies[:3]:
        copy.wait()
    tr, qd = tr_in[...], qd_in[...]
    energy = tr * tr + qd * qd
    own[:, :BLK] = energy
    gain = jnp.concatenate([ga_in[...], ga_in[...]], axis=1)
    gain = jnp.broadcast_to(gain, (128, 128)).T[:ST]
    own[:, BLK:] = gain[:, : 384 - BLK]
    total = jnp.sum(energy, axis=1, keepdims=True)
    total = jnp.broadcast_to(total, (ST, 128))
    total = jnp.concatenate([total, total], axis=0).T[:2]
    hi = total.astype(BF16).astype(F32)
    mid = (total - hi).astype(BF16).astype(F32)
    low = total - hi - mid
    row = lax.broadcasted_iota(jnp.int32, (2, 128), 0)
    lane = lax.broadcasted_iota(jnp.int32, (2, 128), 1)
    sums = jnp.where(row == 0, jnp.where(lane < ST, hi, mid), jnp.where(lane < ST, low, 0.0))
    for j in range(STA):
        body = jnp.where(lane[:1] < ST, lag[32 * j : 32 * j + 16], lag[32 * j + 16 : 32 * j + 32])
        pieces = [body[2 * k : 2 * k + 2] for k in range(8)] + [sums]
        chunk[j] = jnp.concatenate(pieces, axis=1).astype(BF16)


def turn(e0, e1, e2, e3, main, near, far, tall):
    for k, e in enumerate((e0, e1, e2, e3)):
        at = pl.multiple_of((lax.axis_index("sta") ^ k) * ST, ST)
        tall[pl.ds(at, ST), :] = e[...]
    main[...] = tall[...].T
    first, last = main[0:64, :], main[BLK - 64 : BLK, :]
    low_half = lax.axis_index("src") < SRC // STEPS
    near[...] = jnp.where(low_half, first, last)
    far[...] = jnp.where(low_half, last, first)


def beams(received, main, halo, far_halo, power, line, weighted, table, lagged, opened):
    src = lax.axis_index("src")
    middle = SRC // STEPS
    lane = lax.broadcasted_iota(jnp.int32, (1, 128), 1)
    left = lane < ST
    totals = []
    for j in range(STA):
        acc = jnp.zeros((2, 128), F32)
        for i in range(SRC):
            acc = acc + received[STA * i + j, :, 1024:].astype(F32)
        acc = acc[0:1] + acc[1:2]
        totals.append(acc + pltpu.roll(acc, ST, 1))
    halves = [jnp.where(left, totals[0], totals[1]), jnp.where(left, totals[2], totals[3])]
    baseline = jnp.concatenate(halves, axis=1) / SAMPLES
    gain = main[BLK : BLK + 1, :]

    def weigh(energy):
        return (gain * (energy - baseline)).astype(BF16).astype(F32)

    edge = weigh(halo[...] + far_halo[...])

    @pl.when(src < middle)
    def _():
        line[0:264, :] = weigh(main[0:264, :])
        line[BLK : BLK + 64, :] = edge

    @pl.when(src >= middle)
    def _():
        line[0:HALO, :] = edge[1:64]
        line[HALO : HALO + 264, :] = weigh(main[0:264, :])

    for b in range(COPIES):
        weighted[b] = line[b : b + 256 + LAGS - COPIES, :].astype(BF16)
    table[...] = line[256:384, :].T
    extra = [[jnp.zeros((8, 512), F32) for _ in range(2)] for _ in range(2)]
    for j in range(STA):
        for i in range(SRC):
            for k in range(8):
                opened[j, 16 * i + 2 * k : 16 * i + 2 * k + 2, :] = received[
                    STA * i + j, :, 128 * k : 128 * k + 128
                ].astype(F32)
        part = opened[j].T.astype(jnp.int32)
        for h in range(2):
            for row in range(0, ST, 8):
                entry = table[ST * j + row : ST * j + row + 8, :]
                index = part[ST * h + row : ST * h + row + 8]
                for k in range(2):
                    found = [
                        jnp.take_along_axis(entry, index[:, c : c + 128] + k, axis=1, mode="promise_in_bounds")
                        for c in range(0, 512, 128)
                    ]
                    extra[h][k] = extra[h][k] + jnp.concatenate(found, axis=1)
    for t in range(2):
        one, two = opened[2 * t], opened[2 * t + 1]
        lagged[0:512, 128 * t : 128 * t + 128] = jnp.where(left, one, pltpu.roll(two, ST, 1)).astype(BF16)
        lagged[512:, 128 * t : 128 * t + 128] = jnp.where(left, pltpu.roll(one, ST, 1), two).astype(BF16)
    start = jnp.where(src == middle, W - (BLK * middle - HALO), 0)
    stop = jnp.where(src == middle - 1, W - BLK * (middle - 1), jnp.where(src == SRC - 1, BLK - 1, BLK))
    at = lax.broadcasted_iota(jnp.int32, (1, 256), 1)
    inside = jnp.logical_and(at >= start, at < stop)
    lag = lagged[...]
    picks = [jnp.where(lag == BF16(b), BF16(1), BF16(0)) for b in range(LAGS)]
    shifted = [weighted[b % COPIES, b - b % COPIES : b - b % COPIES + 256, :] for b in range(LAGS)]
    beam = lax.dot_general(
        jnp.concatenate(picks, axis=1),
        jnp.concatenate(shifted, axis=1),
        (((1,), (1,)), ((), ())),
        preferred_element_type=F32,
    )
    beam = jnp.where(inside, beam, 0.0)
    squared = beam * beam
    squared = jnp.sum((squared[:, :128] + squared[:, 128:]).T, axis=0, keepdims=True)
    for h in range(2):
        row = squared[:, 512 * h : 512 * h + 512]
        for k in range(2):
            late = jnp.sum(extra[h][k], axis=0, keepdims=True)
            row = row + jnp.where(256 + k < stop, late * late, 0.0)
        for g in range(4):
            power[4 * h + g : 4 * h + g + 1, :] = row[:, 128 * g : 128 * g + 128]


def finish(parts, out, sums):
    src = lax.axis_index("src")
    h = lax.axis_index("sta") % 2
    lane = lax.broadcasted_iota(jnp.int32, (1, 128), 1)
    for k in range(STEPS):
        peak = None
        for j in range(STA):
            acc = parts[k * HALF + j]
            for i in range(1, SRC // STEPS):
                acc = acc + parts[k * HALF + STA * i + j]
            sums[8 * j : 8 * j + 4, :] = acc
            peak = acc if peak is None else jnp.maximum(peak, acc)
        peak = jnp.max(peak, axis=(0, 1), keepdims=True)
        cells = jnp.zeros((1, 128), F32)
        for j in range(STA):
            row = sums[pl.ds(8 * j + src // 8, 1), :]
            to = 32 * j + 16 * h
            row = pltpu.roll(row, (to - 16 * (src % 8) + 128) % 128, 1)
            cells = jnp.where(lane // 16 == 2 * j + h, row, cells)
        out[k : k + 1, :] = cells
        out[STEPS + k : STEPS + k + 1, :] = jnp.broadcast_to(peak, (1, 128))


def call(kernel, out_shape, specs, scratch=()):
    multi = isinstance(out_shape, (list, tuple))
    return pl.pallas_call(
        kernel,
        out_shape=out_shape,
        in_specs=specs,
        out_specs=[VMEM] * len(out_shape) if multi else VMEM,
        scratch_shapes=scratch,
        compiler_params=pltpu.CompilerParams(vmem_limit_bytes=48 << 20),
    )


def shape(dims, dtype=F32):
    return jax.ShapeDtypeStruct(dims, dtype)


def program(trace, quadrature, gains, lags):
    inputs = [pltpu.with_memory_space_constraint(x, pltpu.HBM) for x in (trace, quadrature, gains[None], lags.T)]
    own, chunk = call(
        prologue,
        [shape((ST, 384)), shape((STA, 2, WIDE), BF16)],
        [pl.BlockSpec(memory_space=pltpu.HBM)] * 4,
        [
            pltpu.VMEM((ST, BLK), F32),
            pltpu.VMEM((ST, BLK), F32),
            pltpu.VMEM((1, ST), F32),
            pltpu.VMEM((ST, CPD), jnp.int32),
            pltpu.SemaphoreType.DMA((4,)),
        ],
    )(*inputs)
    blocks = [own]
    for k in range(1, STA):
        blocks.append(lax.ppermute(own, "sta", [(j ^ k, j) for j in range(STA)]))
    chunks = jnp.broadcast_to(chunk[None], (SRC, STA, 2, WIDE)).reshape(DEV, 2, WIDE)
    received = lax.all_to_all(chunks, ("src", "sta"), 0, 0, tiled=True)
    main, near, far = call(
        turn,
        [shape((384, STATIONS)), shape((64, STATIONS)), shape((64, STATIONS))],
        [VMEM] * 4,
        [pltpu.VMEM((STATIONS, 384), F32)],
    )(*blocks)
    middle = SRC // STEPS
    pairs = [(i + 1, i) for i in range(middle - 1)] + [(i - 1, i) for i in range(middle + 1, SRC)]
    halo = lax.ppermute(near, "src", pairs)
    far_halo = lax.ppermute(far, "src", [(middle, middle - 1), (middle - 1, middle)])
    power = call(
        beams,
        shape((8, 128)),
        [VMEM] * 4,
        [
            pltpu.VMEM((384, STATIONS), F32),
            pltpu.VMEM((COPIES, 256 + LAGS - COPIES, STATIONS), BF16),
            pltpu.VMEM((STATIONS, 128), F32),
            pltpu.VMEM((1024, STATIONS), BF16),
            pltpu.VMEM((STA, 512, 128), F32),
        ],
    )(received, main, halo, far_halo)
    halves = jnp.broadcast_to(power.reshape(1, 2, 4, 128), (DEV // 2, 2, 4, 128)).reshape(DEV, 4, 128)
    parts = lax.all_to_all(halves, ("src", "sta"), 0, 0, tiled=True)
    mine = call(finish, shape((2 * STEPS, CPD)), [VMEM], [pltpu.VMEM((32, 128), F32)])(parts)
    other = lax.ppermute(mine, "sta", [(0, 1), (1, 0), (2, 3), (3, 2)])
    cells = mine[:STEPS] + other[:STEPS]
    return cells / jnp.maximum(mine[STEPS:], other[STEPS:])


def solution(mesh):
    return jax.shard_map(
        program,
        mesh=mesh,
        in_specs=(P("sta", "src"), P("sta", "src"), P("sta"), P("src", "sta")),
        out_specs=P(None, "src"),
        check_vma=False,
    )
```
